32 devices in a mesh: group: 2 (over y), seq: 16 (over z, x, core).
Axes of the slice: x: 2, y: 2, z: 4, core: 2. Of those that a mesh axis runs over, the one named last changes fastest.
Arguments:
- coarse_query: bfloat16 [1024, 3072], P(('group', 'seq')), parts along dimension 0, may hold values from -96 to 96
- coarse_key: bfloat16 [1024, 3072], P(('group', 'seq')), parts along dimension 0, may hold values from -12 to 12
- coarse_value: bfloat16 [1024, 3072], P(('group', 'seq')), parts along dimension 0, may hold values from -6 to 6
- fine_query: bfloat16 [4096, 3072], P(('group', 'seq')), parts along dimension 0, may hold values from -108 to 108
- fine_key: bfloat16 [4096, 3072], P(('group', 'seq')), parts along dimension 0, may hold values from -9 to 9
- fine_value: bfloat16 [4096, 3072], P(('group', 'seq')), parts along dimension 0, may hold values from -6 to 6
- head_reach: int32 [24], replicated, may hold values from 1 to 2, as said below
Outputs:
- fine_result: bfloat16 [4096, 3072], P(('group', 'seq')), parts along dimension 0
- cross_result: bfloat16 [4096, 3072], P(('group', 'seq')), parts along dimension 0
The draws below stay inside these ranges and needn't reach their ends.
There are 2 independent parts, one for each index of `group`. The reference program is written for one: setup_inputs(seed, part) draws one part's arguments, and reference() takes and returns one part's arrays. A program takes and returns all parts, laid end to end along the dimension named above; an argument that names none is the same for every part. Nothing has to cross between parts.
Inputs may be any that keep to these rules, and one draw needn't show every extreme that they name: `head_reach`: each head reaches at least one frame; some head reaches 2 frames.
All inputs are finite; a program needn't handle non-finite values.
Results may differ from the reference program's by a relative error of at most 0.0054.
Values may be sent and summed in bfloat16 or wider, within the bound.
No kernel may reach another device: no remote copies, remote signals or barrier semaphores. Data moves between devices by JAX's collectives and lax.ppermute only.
A program may use at most 128 MiB of HBM per device.

```python
import math
import jax
import jax.numpy as jnp
from jax import lax

D = 3072
HEADS = 24
HD = 128
TT = 4
TH = 4
TW = 8
NT = 8
HALO_F = 2
NS = 2
F_DEV = 128
C_DEV = 32
LC = 512
LF = 2048
FRAMES = 32
N_SEQ = 16


def paired_rows(key, row_count, column_count, deviation, variant):
    bound = 6.0 * deviation
    key_noise = jax.random.normal(jax.random.fold_in(key, variant + 1), (row_count, column_count), jnp.float32)
    key_rows = jnp.clip(deviation * key_noise, -bound, bound)
    query_noise = jax.random.normal(jax.random.fold_in(key, variant + 2), (row_count, column_count), jnp.float32)
    queries = jnp.clip(deviation * query_noise, -bound, bound)
    return (queries, key_rows)


def draw_coarse_query(key, part):
    return paired_rows(key, LC, D, 2.0, 100)[0].astype(jnp.bfloat16)


def draw_coarse_key(key, part):
    return paired_rows(key, LC, D, 2.0, 100)[1].astype(jnp.bfloat16)


def draw_fine_query(key, part):
    return paired_rows(key, LF, D, 1.5, 200)[0].astype(jnp.bfloat16)


def draw_fine_key(key, part):
    return paired_rows(key, LF, D, 1.5, 200)[1].astype(jnp.bfloat16)


def draw_head_reach(key, part):
    reaches = jax.random.randint(jax.random.fold_in(key, 301), (HEADS,), 1, HALO_F + 1)
    ordering = jax.random.permutation(jax.random.fold_in(key, 302), HEADS)
    reaches = reaches.at[ordering[0]].set(HALO_F)
    reaches = reaches.at[ordering[1]].set(1)
    return reaches.astype(jnp.int32)


def block_scale(rng, extent, split, least, top_value):
    def one(position, shards_of):
        heights = jax.random.uniform(jax.random.fold_in(jax.random.fold_in(rng, 6), position), (shards_of,), jnp.float32, least / len(split), top_value / len(split))
        return jnp.repeat(jnp.exp(heights), extent[position] // shards_of).reshape((-1,) + (1,) * (len(extent) - position - 1))

    loudness = one(*split[0])
    for cut in split[1:]:
        loudness = loudness * one(*cut)
    return loudness


def bell_draw(own_key, shape, scale, most, pieces=(), kind=jnp.bfloat16):
    drawn = scale * jax.random.normal(own_key, shape, jnp.float32)
    if pieces:
        drawn = drawn * block_scale(own_key, shape, pieces, -0.22, 0.18)
    return jnp.clip(drawn, -most, most).astype(kind)


def setup_inputs(seed: int = 0, part: int = 0) -> dict:
    keys = jax.random.split(jax.random.key(seed), 8)
    part_keys = jax.random.split(jax.random.fold_in(keys[7], part), 8)
    coarse_query = draw_coarse_query(jax.random.fold_in(jax.random.fold_in(keys[7], part), 71), part)
    coarse_key = draw_coarse_key(jax.random.fold_in(jax.random.fold_in(keys[7], part), 71), part)
    coarse_value = bell_draw(part_keys[2], (LC, D), 1.0, 6.0, ((0, 16),))
    fine_query = draw_fine_query(jax.random.fold_in(jax.random.fold_in(keys[7], part), 71), part)
    fine_key = draw_fine_key(jax.random.fold_in(jax.random.fold_in(keys[7], part), 71), part)
    fine_value = bell_draw(part_keys[5], (LF, D), 1.0, 6.0, ((0, 16),))
    head_reach = draw_head_reach(jax.random.fold_in(keys[7], 71), part)
    return {"coarse_query": coarse_query, "coarse_key": coarse_key, "coarse_value": coarse_value, "fine_query": fine_query, "fine_key": fine_key, "fine_value": fine_value, "head_reach": head_reach}


masked_score = -1e30


def softmax_rows(scores):
    largest = jnp.max(scores, axis=-1, keepdims=True)
    exponent = jnp.exp(scores - largest)
    return (exponent / jnp.sum(exponent, axis=-1, keepdims=True)).astype(jnp.bfloat16)


def attend_heads(query_rows, key_rows, value_rows, allowed):
    head_total = query_rows.shape[1] // HD
    query_heads = query_rows.reshape(query_rows.shape[0], head_total, HD).astype(jnp.float32)
    key_heads = key_rows.reshape(key_rows.shape[0], head_total, HD).astype(jnp.float32)
    value_heads = value_rows.reshape(value_rows.shape[0], head_total, HD).astype(jnp.float32)
    scores = jnp.einsum("qhd,khd->hqk", query_heads, key_heads, precision=lax.Precision.HIGHEST) * (HD ** -0.5)
    if allowed is not None:
        scores = jnp.where(allowed, scores, masked_score)
    weights = softmax_rows(scores).astype(jnp.float32)
    blended = jnp.einsum("hqk,khd->qhd", weights, value_heads, precision=lax.Precision.HIGHEST)
    return blended.reshape(query_rows.shape[0], head_total * HD)


def pool_frames(coarse_rows):
    cells = (TH // 2) * (TW // 2)
    summed = jnp.sum(coarse_rows.reshape(-1, cells, D).astype(jnp.float32), axis=1)
    return summed * (cells ** -0.5)


def reference(coarse_query, coarse_key, coarse_value, fine_query, fine_key, fine_value, head_reach):
    block_rows = math.gcd(LC, 1024)

    def one_head(head_index):
        first_column = head_index * HD
        query_columns = lax.dynamic_slice_in_dim(coarse_query, first_column, HD, 1)
        key_columns = lax.dynamic_slice_in_dim(coarse_key, first_column, HD, 1)
        value_columns = lax.dynamic_slice_in_dim(coarse_value, first_column, HD, 1)

        def one_block(query_block):
            scores = jnp.dot(query_block, key_columns.T, preferred_element_type=jnp.float32) * (HD ** -0.5)
            weights = softmax_rows(scores)
            return jnp.dot(weights, value_columns, preferred_element_type=jnp.float32).astype(jnp.bfloat16)

        return lax.map(one_block, query_columns.reshape(LC // block_rows, block_rows, HD)).reshape(LC, HD)

    per_head = lax.map(one_head, jnp.arange(HEADS, dtype=jnp.int32))
    coarse_attention = per_head.transpose(1, 0, 2).reshape(LC, D)
    pooled_key = pool_frames(coarse_key)
    pooled_value = pool_frames(coarse_value)
    plane_cells = TH * TW
    key_tiles = jnp.pad(fine_key.reshape(NT, NS, F_DEV, D), ((1, 1), (0, 0), (0, 0), (0, 0)))
    value_tiles = jnp.pad(fine_value.reshape(NT, NS, F_DEV, D), ((1, 1), (0, 0), (0, 0), (0, 0)))
    query_tiles = fine_query.reshape(N_SEQ, F_DEV, D)
    coarse_tiles = coarse_attention.reshape(N_SEQ, C_DEV, D)
    zero_index = jnp.int32(0)

    def one_tile(tile_index):
        time_block = (tile_index // NS).astype(jnp.int32)
        region = (tile_index % NS).astype(jnp.int32)
        query_rows = lax.dynamic_index_in_dim(query_tiles, tile_index, 0, keepdims=False)
        window_key = lax.dynamic_slice(key_tiles, (time_block, region, zero_index, zero_index), (3, 1, F_DEV, D)).reshape(3 * F_DEV, D)
        window_value = lax.dynamic_slice(value_tiles, (time_block, region, zero_index, zero_index), (3, 1, F_DEV, D)).reshape(3 * F_DEV, D)
        query_frame = time_block * TT + jnp.arange(F_DEV, dtype=jnp.int32) // plane_cells
        key_frame = time_block * TT - TT + jnp.arange(3 * F_DEV, dtype=jnp.int32) // plane_cells
        distance = jnp.abs(query_frame[:, None] - key_frame[None, :])
        inside = (key_frame >= 0) & (key_frame < FRAMES)
        allowed = (distance[None, :, :] <= head_reach[:, None, None]) & inside[None, None, :]
        window_attention = attend_heads(query_rows, window_key, window_value, allowed)
        coarse_rows = lax.dynamic_index_in_dim(coarse_tiles, tile_index, 0, keepdims=False)
        spread = coarse_rows.reshape(TT, TH // 2, 1, TW // 2, 1, D)
        upsampled = jnp.broadcast_to(spread, (TT, TH // 2, 2, TW // 2, 2, D)).reshape(F_DEV, D)
        fine_rows = (window_attention + upsampled.astype(jnp.float32)).astype(jnp.bfloat16)
        cross_rows = attend_heads(query_rows, pooled_key, pooled_value, None).astype(jnp.bfloat16)
        return fine_rows, cross_rows

    fine_tiles, cross_tiles = lax.map(one_tile, jnp.arange(N_SEQ, dtype=jnp.int32))
    return fine_tiles.reshape(LF, D), cross_tiles.reshape(LF, D)
```

```python
import functools
import math

import jax
import jax.numpy as jnp
from jax import lax
from jax.experimental import pallas as pl
from jax.experimental.pallas import tpu as pltpu
from jax.sharding import PartitionSpec as P

HD = 128
TT = 4
TH = 4
TW = 8
NT = 8
HALO_F = 2

PLANE = TH * TW
CELLS = (TH // 2) * (TW // 2)
SCALE = HD**-0.5
MASKED = -1e30
FAR = 1 << 20

VMEM = pl.BlockSpec(memory_space=pltpu.VMEM)
SMEM = pl.BlockSpec(memory_space=pltpu.SMEM)


def softmax_rows(scores):
    exponent = jnp.exp(scores - jnp.max(scores, axis=-1, keepdims=True))
    return (exponent / jnp.sum(exponent, axis=-1, keepdims=True)).astype(jnp.bfloat16)


def dot_rows(left, right):
    return lax.dot_general(left, right, (((1,), (1,)), ((), ())), preferred_element_type=jnp.float32)


def dot_plain(left, right):
    return lax.dot_general(left, right, (((1,), (0,)), ((), ())), preferred_element_type=jnp.float32)


def halo_kernel(place, key_ref, value_ref, out_ref):
    rows = key_ref.shape[0]
    out_ref[:rows] = key_ref[...]
    out_ref[rows:] = value_ref[...]


def pack_halo(place, fine_key, fine_value, which):
    rows, width = fine_key.shape
    edge = HALO_F * PLANE
    half = rows // edge - 1
    columns = 768
    edge_spec = pl.BlockSpec((edge, columns), lambda c, p: (p[which] * half, c))
    return pl.pallas_call(
        halo_kernel,
        out_shape=jax.ShapeDtypeStruct((2 * edge, width), fine_key.dtype),
        grid_spec=pltpu.PrefetchScalarGridSpec(
            num_scalar_prefetch=1,
            grid=(width // columns,),
            in_specs=[edge_spec, edge_spec],
            out_specs=pl.BlockSpec((2 * edge, columns), lambda c, p: (0, c)),
        ),
        name="pack_halo",
    )(place, fine_key, fine_value)


def pool_rows(rows):
    cells = rows.astype(jnp.float32).reshape(-1, CELLS, rows.shape[1])
    return jnp.sum(cells, axis=1) * CELLS**-0.5


def coarse_pack_kernel(query_ref, key_ref, value_ref, out_ref, pooled_ref):
    rows = query_ref.shape[0]
    for index, ref in enumerate((query_ref, key_ref, value_ref)):
        out_ref[0, index * rows : (index + 1) * rows] = ref[...]
    pooled_ref[:TT] = pool_rows(key_ref[...])
    pooled_ref[TT:] = pool_rows(value_ref[...])


def pack_coarse(coarse_query, coarse_key, coarse_value, groups):
    rows, width = coarse_query.shape
    group_width = width // groups
    column = pl.BlockSpec((rows, group_width), lambda g: (0, g))
    return pl.pallas_call(
        coarse_pack_kernel,
        out_shape=(
            jax.ShapeDtypeStruct((groups, 3 * rows, group_width), coarse_query.dtype),
            jax.ShapeDtypeStruct((2 * TT, width), jnp.float32),
        ),
        grid=(groups,),
        in_specs=[column, column, column],
        out_specs=(
            pl.BlockSpec((1, 3 * rows, group_width), lambda g: (g, 0, 0)),
            pl.BlockSpec((2 * TT, group_width), lambda g: (0, g)),
        ),
        name="pack_coarse",
    )(coarse_query, coarse_key, coarse_value)


def split_pooled_kernel(*refs):
    *in_refs, out_ref = refs
    keys = jnp.concatenate([ref[:TT] for ref in in_refs], axis=0)
    values = jnp.concatenate([ref[TT:] for ref in in_refs], axis=0)
    count = keys.shape[0]
    high = keys.astype(jnp.bfloat16).astype(jnp.float32)
    low = keys - high
    out_ref[...] = jnp.concatenate([high, low, values], axis=0).astype(jnp.bfloat16)


def split_pooled(pieces):
    width = pieces[0].shape[1]
    return pl.pallas_call(
        split_pooled_kernel,
        out_shape=jax.ShapeDtypeStruct((3 * TT * len(pieces), width), jnp.bfloat16),
        in_specs=[VMEM] * len(pieces),
        out_specs=VMEM,
        name="split_pooled",
    )(*pieces)


def coarse_kernel(own_ref, *refs):
    *other_refs, out_ref = refs
    members, packed, _ = own_ref.shape
    rows = packed // 3

    def flat(ref, start):
        piece = ref[:, start : start + rows]
        return piece.reshape(members * rows, HD)

    query = flat(own_ref, 0)
    keys = jnp.concatenate([flat(own_ref, rows)] + [flat(r, 0) for r in other_refs], axis=0)
    values = jnp.concatenate([flat(own_ref, 2 * rows)] + [flat(r, rows) for r in other_refs], axis=0)
    weights = softmax_rows(dot_rows(query, keys) * SCALE)
    mixed = dot_plain(weights, values)
    out_ref[...] = mixed.astype(out_ref.dtype).reshape(members, rows, HD)


def attend_coarse(own, others):
    members, packed, group_width = own.shape
    rows = packed // 3
    return pl.pallas_call(
        coarse_kernel,
        out_shape=jax.ShapeDtypeStruct((members, rows, group_width), own.dtype),
        grid=(group_width // HD,),
        in_specs=[pl.BlockSpec((members, packed, HD), lambda h: (0, 0, h))]
        + [pl.BlockSpec((members, 2 * rows, HD), lambda h: (0, 0, h)) for _ in others],
        out_specs=pl.BlockSpec((members, rows, HD), lambda h: (0, 0, h)),
        name="attend_coarse",
    )(own, *others)


def cross_kernel(chunk, query_ref, *refs):
    *token_refs, out_ref = refs
    third = chunk // 3
    high, low, values = [], [], []
    for ref in token_refs:
        rows = ref[...].astype(jnp.float32)
        for start in range(0, rows.shape[0], chunk):
            high.append(rows[start : start + third])
            low.append(rows[start + third : start + 2 * third])
            values.append(rows[start + 2 * third : start + chunk])
    high = jnp.concatenate(high, axis=0).astype(jnp.bfloat16)
    low = jnp.concatenate(low, axis=0).astype(jnp.bfloat16)
    values = jnp.concatenate(values, axis=0).astype(jnp.bfloat16)
    for head in range(query_ref.shape[1] // HD):
        cut = slice(head * HD, (head + 1) * HD)
        query = query_ref[:, cut]
        scores = dot_rows(
            jnp.concatenate([query, query], axis=1),
            jnp.concatenate([high[:, cut], low[:, cut]], axis=1),
        )
        weights = softmax_rows(scores * SCALE)
        out_ref[:, cut] = dot_plain(weights, values[:, cut]).astype(out_ref.dtype)


def attend_cross(fine_query, tokens, chunk, heads_at_once):
    rows, width = fine_query.shape
    columns = heads_at_once * HD
    return pl.pallas_call(
        functools.partial(cross_kernel, chunk),
        out_shape=jax.ShapeDtypeStruct((rows, width), jnp.bfloat16),
        grid=(width // columns,),
        in_specs=[pl.BlockSpec((rows, columns), lambda c: (0, c))]
        + [pl.BlockSpec((t.shape[0], columns), lambda c: (0, c)) for t in tokens],
        out_specs=pl.BlockSpec((rows, columns), lambda c: (0, c)),
        name="attend_cross",
    )(fine_query, *tokens)


def window_kernel(place, reach, query_ref, key_ref, value_ref, pair_ref, next_ref, out_ref):
    rows, columns = query_ref.shape
    edge = HALO_F * PLANE
    total = rows + 2 * edge
    time_tile = place[2]
    later = time_tile % 2 == 0
    row_frame = lax.broadcasted_iota(jnp.int32, (rows, total), 0) // PLANE
    column = lax.broadcasted_iota(jnp.int32, (rows, total), 1)
    own_frame = column // PLANE
    pair_frame = (column - rows) // PLANE + jnp.where(later, TT, -HALO_F)
    next_frame = (column - rows - edge) // PLANE + jnp.where(later, -HALO_F, TT)
    key_frame = jnp.where(column < rows, own_frame, jnp.where(column < rows + edge, pair_frame, next_frame))
    distance = jnp.abs(row_frame - key_frame)
    absolute = key_frame + time_tile * TT
    distance = jnp.where((absolute >= 0) & (absolute < NT * TT), distance, FAR)
    first_head = pl.program_id(0) * (columns // HD)
    for head in range(columns // HD):
        cut = slice(head * HD, (head + 1) * HD)
        keys = jnp.concatenate([key_ref[:, cut], pair_ref[:edge, cut], next_ref[:edge, cut]], axis=0)
        values = jnp.concatenate([value_ref[:, cut], pair_ref[edge:, cut], next_ref[edge:, cut]], axis=0)
        scores = dot_rows(query_ref[:, cut], keys) * SCALE
        scores = jnp.where(distance <= reach[first_head + head], scores, MASKED)
        out_ref[:, cut] = dot_plain(softmax_rows(scores), values)


def attend_window(place, head_reach, fine_query, fine_key, fine_value, pair, beyond, heads_at_once):
    rows, width = fine_query.shape
    columns = heads_at_once * HD
    block = pl.BlockSpec((rows, columns), lambda c, p, r: (0, c))
    halo = pl.BlockSpec((pair.shape[0], columns), lambda c, p, r: (0, c))
    return pl.pallas_call(
        window_kernel,
        out_shape=jax.ShapeDtypeStruct((rows, width), jnp.float32),
        grid_spec=pltpu.PrefetchScalarGridSpec(
            num_scalar_prefetch=2,
            grid=(width // columns,),
            in_specs=[block, block, block, halo, halo],
            out_specs=block,
        ),
        name="attend_window",
    )(place, head_reach, fine_query, fine_key, fine_value, pair, beyond)


def finish_kernel(window_ref, coarse_ref, out_ref):
    rows = window_ref.shape[0]
    coarse_rows = coarse_ref.shape[1]
    row = lax.broadcasted_iota(jnp.int32, (rows, coarse_rows), 0)
    column = lax.broadcasted_iota(jnp.int32, (rows, coarse_rows), 1)
    frame, y, x = row // PLANE, (row % PLANE) // TW, row % TW
    source = frame * CELLS + (y // 2) * (TW // 2) + x // 2
    pick = (source == column).astype(jnp.bfloat16)
    upsampled = dot_plain(pick, coarse_ref[0])
    out_ref[...] = (window_ref[...] + upsampled).astype(out_ref.dtype)


def finish(window, returned):
    rows, width = window.shape
    groups, coarse_rows, group_width = returned.shape
    block = pl.BlockSpec((rows, group_width), lambda g: (0, g))
    return pl.pallas_call(
        finish_kernel,
        out_shape=jax.ShapeDtypeStruct((rows, width), jnp.bfloat16),
        grid=(groups,),
        in_specs=[block, pl.BlockSpec((1, coarse_rows, group_width), lambda g: (g, 0, 0))],
        out_specs=block,
        name="finish",
    )(window, returned)


def shards(coarse_query, coarse_key, coarse_value, fine_query, fine_key, fine_value, head_reach):
    devices = lax.axis_size("seq")
    position = lax.axis_index("seq")
    head_count = coarse_query.shape[1] // HD
    groups = math.gcd(head_count, devices)
    blocks = devices // groups
    inner = math.gcd(2, groups)
    outer = groups // inner
    tiles_across = devices // NT
    time_tile = position // tiles_across

    def seat(o, b, c):
        return (o * blocks + b) * inner + c

    def around(value, extent, move):
        moved = []
        for step in range(1, extent):
            links = [
                (seat(o, b, c), seat(*move(o, b, c, step)))
                for o in range(outer)
                for b in range(blocks)
                for c in range(inner)
            ]
            moved.append(lax.ppermute(value, "seq", links))
        return moved

    over_blocks = functools.partial(around, extent=blocks, move=lambda o, b, c, s: (o, (b + s) % blocks, c))
    over_outer = functools.partial(around, extent=outer, move=lambda o, b, c, s: ((o + s) % outer, b, c))
    over_inner = functools.partial(around, extent=inner, move=lambda o, b, c, s: (o, b, (c + s) % inner))
    same_block = [[seat(o, b, c) for o in range(outer) for c in range(inner)] for b in range(blocks)]

    def exchange(slots):
        return lax.all_to_all(slots, "seq", 0, 0, tiled=True, axis_index_groups=same_block)

    odd = time_tile % 2
    place = jnp.stack([1 - odd, odd, time_tile]).astype(jnp.int32)
    pairs = [(j, j + tiles_across) for j in range(devices - tiles_across)]
    early = [(a, b) for a, b in pairs if (a // tiles_across) % 2 == 0]
    late = [(a, b) for a, b in pairs if (a // tiles_across) % 2 == 1]

    def swap(value, links):
        return lax.ppermute(value, "seq", links + [(b, a) for a, b in links])

    pair = swap(pack_halo(place, fine_key, fine_value, 0), early)
    slots, pooled = pack_coarse(coarse_query, coarse_key, coarse_value, groups)
    received = exchange(slots)
    beyond = swap(pack_halo(place, fine_key, fine_value, 1), late)
    token_part = split_pooled([pooled] + over_blocks(pooled))
    tokens = jnp.concatenate([token_part] + over_outer(token_part), axis=0)
    all_tokens = [tokens] + over_inner(tokens)
    coarse_rows = coarse_query.shape[0]
    attended = attend_coarse(received, over_blocks(received[:, coarse_rows:]))
    returned = exchange(attended)
    cross_result = attend_cross(fine_query, all_tokens, token_part.shape[0], 4)
    window = attend_window(place, head_reach, fine_query, fine_key, fine_value, pair, beyond, 4)
    fine_result = finish(window, returned)
    return (fine_result, cross_result)


def solution(mesh):
    rows = P(("group", "seq"), None)
    return jax.shard_map(
        shards, mesh=mesh, in_specs=(rows,) * 6 + (P(),), out_specs=(rows, rows), check_vma=False
    )
```

```python
import functools
import math

import jax
import jax.numpy as jnp
from jax import lax
from jax.experimental import pallas as pl
from jax.experimental.pallas import tpu as pltpu
from jax.sharding import PartitionSpec as P


HD = 128
TT = 4
TH = 4
TW = 8
NT = 8
HALO_F = 2

PLANE = TH * TW
CELLS = (TH // 2) * (TW // 2)
SCALE = HD**-0.5
MASKED = -1e30
FAR = 1 << 20
GRANT = pltpu.CompilerParams(vmem_limit_bytes=20 << 20)

VMEM = pl.BlockSpec(memory_space=pltpu.VMEM)
SMEM = pl.BlockSpec(memory_space=pltpu.SMEM)
HBM = pl.BlockSpec(memory_space=pltpu.HBM)


def streamed(value):
    return pltpu.with_memory_space_constraint(value, pltpu.HBM)


def dot_rows(left, right):
    return lax.dot_general(left, right, (((1,), (1,)), ((), ())), preferred_element_type=jnp.float32)


def dot_plain(left, right):
    return lax.dot_general(left, right, (((1,), (0,)), ((), ())), preferred_element_type=jnp.float32)


def blend(scores, values):
    exponent = jnp.exp(scores - jnp.max(scores, axis=-1, keepdims=True)).astype(jnp.bfloat16)
    ones = jnp.ones((values.shape[0], HD), values.dtype)
    sums = dot_plain(exponent, jnp.concatenate([values, ones], axis=1))
    return sums[:, :HD] * (1.0 / sums[:, HD:])


def head_cut(head):
    return slice(head * HD, (head + 1) * HD)


def pool_rows(rows):
    cells = rows.astype(jnp.float32).reshape(-1, CELLS, rows.shape[1])
    return jnp.sum(cells, axis=1) * CELLS**-0.5


def pack_kernel(
    tiles_across,
    query_hbm,
    key_hbm,
    value_hbm,
    fine_key_hbm,
    fine_value_hbm,
    slots_hbm,
    pooled_ref,
    pair_hbm,
    far_hbm,
    coarse_buf,
    fine_buf,
    in_sem,
    slot_sem,
    edge_sem,
):
    groups = slots_hbm.shape[0]
    rows, width = query_hbm.shape
    fine_rows = fine_key_hbm.shape[0]
    group_width = width // groups
    edge = HALO_F * PLANE
    odd = (lax.axis_index("seq") // tiles_across) % 2
    loads = []
    for index, source in enumerate((fine_key_hbm, fine_value_hbm)):
        loads.append(pltpu.make_async_copy(source, fine_buf.at[index], in_sem.at[index]))
    for index, source in enumerate((query_hbm, key_hbm, value_hbm)):
        loads.append(pltpu.make_async_copy(source, coarse_buf.at[index], in_sem.at[2 + index]))
    for load in loads:
        load.start()
    stores = []
    for index in range(2):
        loads[index].wait()
        for side, (target, last) in enumerate(((pair_hbm, 1 - odd), (far_hbm, odd))):
            start = pl.multiple_of(last * (fine_rows - edge), edge)
            stores.append(
                pltpu.make_async_copy(
                    fine_buf.at[index, pl.ds(start, edge)],
                    target.at[pl.ds(index * edge, edge)],
                    edge_sem.at[index, side],
                )
            )
            stores[-1].start()
    for index in range(3):
        loads[2 + index].wait()
        for group in range(groups):
            stores.append(
                pltpu.make_async_copy(
                    coarse_buf.at[index, :, pl.ds(group * group_width, group_width)],
                    slots_hbm.at[group, pl.ds(index * rows, rows)],
                    slot_sem.at[index, group],
                )
            )
            stores[-1].start()
    pooled_ref[:TT] = pool_rows(coarse_buf[1])
    pooled_ref[TT:] = pool_rows(coarse_buf[2])
    for store in stores:
        store.wait()


def pack(coarse_query, coarse_key, coarse_value, fine_key, fine_value, groups, tiles_across):
    rows, width = coarse_query.shape
    kind = coarse_query.dtype
    halo = pltpu.HBM((2 * HALO_F * PLANE, width), kind)
    return pl.pallas_call(
        functools.partial(pack_kernel, tiles_across),
        out_shape=(
            pltpu.HBM((groups, 3 * rows, width // groups), kind),
            jax.ShapeDtypeStruct((2 * TT, width), jnp.float32),
            halo,
            halo,
        ),
        in_specs=[HBM] * 5,
        out_specs=(HBM, VMEM, HBM, HBM),
        scratch_shapes=[
            pltpu.VMEM((3, rows, width), kind),
            pltpu.VMEM((2,) + fine_key.shape, kind),
            pltpu.SemaphoreType.DMA((5,)),
            pltpu.SemaphoreType.DMA((3, groups)),
            pltpu.SemaphoreType.DMA((2, 2)),
        ],
        compiler_params=GRANT,
        name="pack",
    )(*map(streamed, (coarse_query, coarse_key, coarse_value, fine_key, fine_value)))


def split_pooled_kernel(*refs):
    *in_refs, out_ref = refs
    keys = jnp.concatenate([ref[:TT] for ref in in_refs], axis=0)
    values = jnp.concatenate([ref[TT:] for ref in in_refs], axis=0)
    high = keys.astype(jnp.bfloat16).astype(jnp.float32)
    out_ref[...] = jnp.concatenate([high, keys - high, values], axis=0).astype(jnp.bfloat16)


def split_pooled(pieces):
    width = pieces[0].shape[1]
    return pl.pallas_call(
        split_pooled_kernel,
        out_shape=jax.ShapeDtypeStruct((3 * TT * len(pieces), width), jnp.bfloat16),
        in_specs=[VMEM] * len(pieces),
        out_specs=VMEM,
        compiler_params=GRANT,
        name="split_pooled",
    )(*pieces)


def coarse_kernel(own_ref, *refs):
    *other_refs, out_ref = refs
    members, packed, group_width = own_ref.shape
    rows = packed // 3
    for head in range(group_width // HD):
        cut = head_cut(head)

        def flat(ref, start):
            return ref[:, start : start + rows, cut].reshape(members * rows, HD)

        query = flat(own_ref, 0)
        keys = jnp.concatenate([flat(own_ref, rows)] + [flat(r, 0) for r in other_refs], axis=0)
        values = jnp.concatenate([flat(own_ref, 2 * rows)] + [flat(r, rows) for r in other_refs], axis=0)
        mixed = blend(dot_rows(query, keys) * SCALE, values)
        out_ref[:, :, cut] = mixed.astype(out_ref.dtype).reshape(members, rows, HD)


def attend_coarse(own, others):
    members, packed, group_width = own.shape
    return pl.pallas_call(
        coarse_kernel,
        out_shape=jax.ShapeDtypeStruct((members, packed // 3, group_width), own.dtype),
        in_specs=[VMEM] * (1 + len(others)),
        out_specs=VMEM,
        compiler_params=GRANT,
        name="attend_coarse",
    )(own, *others)


def cross_kernel(chunk, query_ref, *refs):
    *token_refs, out_ref = refs
    third = chunk // 3
    for head in range(query_ref.shape[1] // HD):
        cut = head_cut(head)
        high, low, values = [], [], []
        for ref in token_refs:
            rows = ref[:, cut].astype(jnp.float32)
            for start in range(0, rows.shape[0], chunk):
                high.append(rows[start : start + third])
                low.append(rows[start + third : start + 2 * third])
                values.append(rows[start + 2 * third : start + chunk])
        high, low, values = (jnp.concatenate(p, axis=0).astype(jnp.bfloat16) for p in (high, low, values))
        query = query_ref[:, cut]
        scores = dot_rows(jnp.concatenate([query, query], axis=1), jnp.concatenate([high, low], axis=1))
        out_ref[:, cut] = blend(scores * SCALE, values).astype(out_ref.dtype)


def attend_cross(fine_query, tokens, chunk):
    return pl.pallas_call(
        functools.partial(cross_kernel, chunk),
        out_shape=jax.ShapeDtypeStruct(fine_query.shape, jnp.bfloat16),
        in_specs=[VMEM] * (1 + len(tokens)),
        out_specs=VMEM,
        compiler_params=GRANT,
        name="attend_cross",
    )(fine_query, *tokens)


def window_kernel(tiles_across, reach, query_ref, key_ref, value_ref, pair_ref, far_ref, out_ref, bias):
    rows, width = query_ref.shape
    edge = HALO_F * PLANE
    total = rows + 2 * edge
    time_tile = lax.axis_index("seq") // tiles_across
    later = time_tile % 2 == 0
    row_frame = lax.broadcasted_iota(jnp.int32, (rows, total), 0) // PLANE
    column = lax.broadcasted_iota(jnp.int32, (rows, total), 1)
    pair_frame = (column - rows) // PLANE + jnp.where(later, TT, -HALO_F)
    far_frame = (column - rows - edge) // PLANE + jnp.where(later, -HALO_F, TT)
    key_frame = jnp.where(column < rows, column // PLANE, jnp.where(column < rows + edge, pair_frame, far_frame))
    absolute = key_frame + time_tile * TT
    distance = jnp.where((absolute >= 0) & (absolute < NT * TT), jnp.abs(row_frame - key_frame), FAR)
    for limit in range(HALO_F):
        bias[limit] = jnp.where(distance <= limit + 1, 0.0, MASKED)
    for head in range(width // HD):
        cut = head_cut(head)
        keys = jnp.concatenate([key_ref[:, cut], pair_ref[:edge, cut], far_ref[:edge, cut]], axis=0)
        values = jnp.concatenate([value_ref[:, cut], pair_ref[edge:, cut], far_ref[edge:, cut]], axis=0)
        scores = dot_rows(query_ref[:, cut], keys) * SCALE + bias[reach[head] - 1]
        out_ref[:, cut] = blend(scores, values)


def attend_window(head_reach, fine_query, fine_key, fine_value, pair, far, tiles_across):
    rows, width = fine_query.shape
    return pl.pallas_call(
        functools.partial(window_kernel, tiles_across),
        out_shape=jax.ShapeDtypeStruct((rows, width), jnp.float32),
        in_specs=[SMEM] + [VMEM] * 5,
        out_specs=VMEM,
        scratch_shapes=[pltpu.VMEM((HALO_F, rows, 2 * rows), jnp.float32)],
        compiler_params=GRANT,
        name="attend_window",
    )(head_reach, fine_query, fine_key, fine_value, pair, far)


def finish_kernel(window_ref, coarse_ref, out_ref):
    rows = window_ref.shape[0]
    groups, coarse_rows, group_width = coarse_ref.shape
    row = lax.broadcasted_iota(jnp.int32, (rows, coarse_rows), 0)
    column = lax.broadcasted_iota(jnp.int32, (rows, coarse_rows), 1)
    frame, y, x = row // PLANE, (row % PLANE) // TW, row % TW
    source = frame * CELLS + (y // 2) * (TW // 2) + x // 2
    pick = (source == column).astype(jnp.bfloat16)
    for group in range(groups):
        cut = slice(group * group_width, (group + 1) * group_width)
        out_ref[:, cut] = (window_ref[:, cut] + dot_plain(pick, coarse_ref[group])).astype(out_ref.dtype)


def finish(window, returned):
    return pl.pallas_call(
        finish_kernel,
        out_shape=jax.ShapeDtypeStruct(window.shape, jnp.bfloat16),
        in_specs=[VMEM, VMEM],
        out_specs=VMEM,
        compiler_params=GRANT,
        name="finish",
    )(window, returned)


def shards(coarse_query, coarse_key, coarse_value, fine_query, fine_key, fine_value, head_reach):
    devices = lax.axis_size("seq")
    head_count = coarse_query.shape[1] // HD
    groups = math.gcd(head_count, devices)
    blocks = devices // groups
    inner = math.gcd(2, groups)
    outer = groups // inner
    tiles_across = devices // NT

    def seat(o, b, c):
        return (o * blocks + b) * inner + c

    def around(value, extent, move):
        moved = []
        for step in range(1, extent):
            links = [
                (seat(o, b, c), seat(*move(o, b, c, step)))
                for o in range(outer)
                for b in range(blocks)
                for c in range(inner)
            ]
            moved.append(lax.ppermute(value, "seq", links))
        return moved

    over_blocks = functools.partial(around, extent=blocks, move=lambda o, b, c, s: (o, (b + s) % blocks, c))
    over_outer = functools.partial(around, extent=outer, move=lambda o, b, c, s: ((o + s) % outer, b, c))
    over_inner = functools.partial(around, extent=inner, move=lambda o, b, c, s: (o, b, (c + s) % inner))
    same_block = [[seat(o, b, c) for o in range(outer) for c in range(inner)] for b in range(blocks)]

    def exchange(slots):
        return lax.all_to_all(slots, "seq", 0, 0, tiled=True, axis_index_groups=same_block)

    edges = [(j, j + tiles_across) for j in range(devices - tiles_across)]
    early = [(a, b) for a, b in edges if (a // tiles_across) % 2 == 0]
    late = [(a, b) for a, b in edges if (a // tiles_across) % 2 == 1]

    def swap(value, links):
        return lax.ppermute(value, "seq", links + [(b, a) for a, b in links])

    slots, pooled, pair_edge, far_edge = pack(
        coarse_query, coarse_key, coarse_value, fine_key, fine_value, groups, tiles_across
    )
    pair = swap(pair_edge, early)
    received = exchange(slots)
    pieces = [pooled] + over_blocks(pooled)
    token_part = split_pooled(pieces)
    pieces = [token_part] + over_outer(token_part)
    tokens = jnp.concatenate(pieces, axis=0)
    all_tokens = [tokens] + over_inner(tokens)
    coarse_rows = coarse_query.shape[0]
    coarse_keys = received[:, coarse_rows:]
    others = over_blocks(coarse_keys)
    far = swap(far_edge, late)
    cross_result = attend_cross(fine_query, all_tokens, token_part.shape[0])
    attended = attend_coarse(received, others)
    returned = exchange(attended)
    window = attend_window(head_reach, fine_query, fine_key, fine_value, pair, far, tiles_across)
    fine_result = finish(window, returned)
    return (fine_result, cross_result)


def solution(mesh):
    rows = P(("group", "seq"), None)
    return jax.shard_map(
        shards, mesh=mesh, in_specs=(rows,) * 6 + (P(),), out_specs=(rows, rows), check_vma=False
    )
```

```python
import functools
import math

import jax
import jax.numpy as jnp
from jax import lax
from jax.experimental import pallas as pl
from jax.experimental.pallas import tpu as pltpu
from jax.sharding import PartitionSpec as P


HD = 128
TT = 4
TH = 4
TW = 8
NT = 8
HALO_F = 2

PLANE = TH * TW
CELLS = (TH // 2) * (TW // 2)
SCALE = HD**-0.5
MASKED = -1e30
FAR = 1 << 20
GRANT = pltpu.CompilerParams(vmem_limit_bytes=12 << 20)


VMEM = pl.BlockSpec(memory_space=pltpu.VMEM)
SMEM = pl.BlockSpec(memory_space=pltpu.SMEM)
HBM = pl.BlockSpec(memory_space=pltpu.HBM)
ANY = pl.BlockSpec(memory_space=pl.ANY)


def streamed(value):
    return pltpu.with_memory_space_constraint(value, pltpu.HBM)


def resident(value):
    return pltpu.with_memory_space_constraint(value, pltpu.VMEM)


def dot_rows(left, right):
    return lax.dot_general(left, right, (((1,), (1,)), ((), ())), preferred_element_type=jnp.float32)


def dot_plain(left, right):
    return lax.dot_general(left, right, (((1,), (0,)), ((), ())), preferred_element_type=jnp.float32)


def blend(scores, values):
    exponent = jnp.exp(scores - jnp.max(scores, axis=-1, keepdims=True)).astype(jnp.bfloat16)
    ones = jnp.ones((values.shape[0], HD), values.dtype)
    sums = dot_plain(exponent, jnp.concatenate([values, ones], axis=1))
    return sums[:, :HD] * (1.0 / sums[:, HD:])


def head_cut(head):
    return slice(head * HD, (head + 1) * HD)


def pool_rows(rows):
    cells = rows.astype(jnp.float32).reshape(-1, CELLS, rows.shape[1])
    return jnp.sum(cells, axis=1) * CELLS**-0.5


def pack_kernel(
    tiles_across,
    query_hbm,
    key_hbm,
    value_hbm,
    fine_key_hbm,
    fine_value_hbm,
    slots_hbm,
    pooled_ref,
    pair_key_hbm,
    pair_value_hbm,
    far_key_hbm,
    far_value_hbm,
    coarse_buf,
    fine_buf,
    in_sem,
    slot_sem,
    edge_sem,
):
    groups = slots_hbm.shape[0]
    rows, width = query_hbm.shape
    fine_rows = fine_key_hbm.shape[0]
    group_width = width // groups
    edge = HALO_F * PLANE
    odd = (lax.axis_index("seq") // tiles_across) % 2
    loads = []
    for index, source in enumerate((fine_key_hbm, fine_value_hbm)):
        loads.append(pltpu.make_async_copy(source, fine_buf.at[index], in_sem.at[index]))
    for index, source in enumerate((query_hbm, key_hbm, value_hbm)):
        loads.append(pltpu.make_async_copy(source, coarse_buf.at[index], in_sem.at[2 + index]))
    for load in loads:
        load.start()
    stores = []
    for index in range(2):
        loads[index].wait()
        pair_hbm, far_hbm = ((pair_key_hbm, far_key_hbm), (pair_value_hbm, far_value_hbm))[index]
        for side, (target, last) in enumerate(((pair_hbm, 1 - odd), (far_hbm, odd))):
            start = pl.multiple_of(last * (fine_rows - edge), edge)
            stores.append(
                pltpu.make_async_copy(
                    fine_buf.at[index, pl.ds(start, edge)], target, edge_sem.at[index, side]
                )
            )
            stores[-1].start()
    for index in range(3):
        loads[2 + index].wait()
        for group in range(groups):
            stores.append(
                pltpu.make_async_copy(
                    coarse_buf.at[index, :, pl.ds(group * group_width, group_width)],
                    slots_hbm.at[group, pl.ds(index * rows, rows)],
                    slot_sem.at[index, group],
                )
            )
            stores[-1].start()
    pooled_ref[:TT] = pool_rows(coarse_buf[1])
    pooled_ref[TT:] = pool_rows(coarse_buf[2])
    for store in stores:
        store.wait()


def pack(coarse_query, coarse_key, coarse_value, fine_key, fine_value, groups, tiles_across):
    rows, width = coarse_query.shape
    kind = coarse_query.dtype
    halo = pltpu.HBM((HALO_F * PLANE, width), kind)
    return pl.pallas_call(
        functools.partial(pack_kernel, tiles_across),
        out_shape=(
            pltpu.HBM((groups, 3 * rows, width // groups), kind),
            jax.ShapeDtypeStruct((2 * TT, width), jnp.float32),
            halo,
            halo,
            halo,
            halo,
        ),
        in_specs=[HBM] * 5,
        out_specs=(HBM, VMEM, HBM, HBM, HBM, HBM),
        scratch_shapes=[
            pltpu.VMEM((3, rows, width), kind),
            pltpu.VMEM((2,) + fine_key.shape, kind),
            pltpu.SemaphoreType.DMA((5,)),
            pltpu.SemaphoreType.DMA((3, groups)),
            pltpu.SemaphoreType.DMA((2, 2)),
        ],
        compiler_params=GRANT,
        name="pack",
    )(*map(streamed, (coarse_query, coarse_key, coarse_value, fine_key, fine_value)))


def split_pooled_kernel(*refs):
    *in_refs, out_ref = refs
    keys = jnp.concatenate([ref[:TT] for ref in in_refs], axis=0)
    values = jnp.concatenate([ref[TT:] for ref in in_refs], axis=0)
    high = keys.astype(jnp.bfloat16).astype(jnp.float32)
    out_ref[...] = jnp.concatenate([high, keys - high, values], axis=0).astype(jnp.bfloat16)


def split_pooled(pieces):
    width = pieces[0].shape[1]
    return pl.pallas_call(
        split_pooled_kernel,
        out_shape=jax.ShapeDtypeStruct((3 * TT * len(pieces), width), jnp.bfloat16),
        in_specs=[VMEM] * len(pieces),
        out_specs=VMEM,
        compiler_params=GRANT,
        name="split_pooled",
    )(*pieces)


def coarse_kernel(own_ref, *refs):
    *other_refs, out_ref = refs
    members, packed, group_width = own_ref.shape
    rows = packed // 3
    for head in range(group_width // HD):
        cut = head_cut(head)

        def flat(ref, start):
            return ref[:, start : start + rows, cut].reshape(members * rows, HD)

        query = flat(own_ref, 0)
        keys = jnp.concatenate([flat(own_ref, rows)] + [flat(r, 0) for r in other_refs], axis=0)
        values = jnp.concatenate([flat(own_ref, 2 * rows)] + [flat(r, rows) for r in other_refs], axis=0)
        mixed = blend(dot_rows(query, keys) * SCALE, values)
        out_ref[:, :, cut] = mixed.astype(out_ref.dtype).reshape(members, rows, HD)


def attend_coarse(own, others):
    members, packed, group_width = own.shape
    return pl.pallas_call(
        coarse_kernel,
        out_shape=jax.ShapeDtypeStruct((members, packed // 3, group_width), own.dtype),
        in_specs=[VMEM] * (1 + len(others)),
        out_specs=VMEM,
        compiler_params=GRANT,
        name="attend_coarse",
    )(own, *others)


def cross_kernel(chunk, query_ref, *refs):
    *token_refs, out_ref = refs
    third = chunk // 3
    for head in range(query_ref.shape[1] // HD):
        cut = head_cut(head)
        high, low, values = [], [], []
        for ref in token_refs:
            rows = ref[:, cut].astype(jnp.float32)
            for start in range(0, rows.shape[0], chunk):
                high.append(rows[start : start + third])
                low.append(rows[start + third : start + 2 * third])
                values.append(rows[start + 2 * third : start + chunk])
        high, low, values = (jnp.concatenate(p, axis=0).astype(jnp.bfloat16) for p in (high, low, values))
        query = query_ref[:, cut]
        scores = dot_rows(jnp.concatenate([query, query], axis=1), jnp.concatenate([high, low], axis=1))
        out_ref[:, cut] = blend(scores * SCALE, values).astype(out_ref.dtype)


def attend_cross(fine_query, tokens, chunk):
    rows, width = fine_query.shape
    columns = width // 2 if width % (2 * HD) == 0 else width
    return pl.pallas_call(
        functools.partial(cross_kernel, chunk),
        out_shape=jax.ShapeDtypeStruct(fine_query.shape, jnp.bfloat16),
        grid=(width // columns,),
        in_specs=[pl.BlockSpec((t.shape[0], columns), lambda c: (0, c)) for t in (fine_query, *tokens)],
        out_specs=pl.BlockSpec((rows, columns), lambda c: (0, c)),
        compiler_params=GRANT,
        name="attend_cross",
    )(streamed(fine_query), *tokens)


def window_kernel(tiles_across, reach, *refs):
    *sources, out_ref, held, edges, bias, sem = refs
    rows, width = out_ref.shape
    parts, columns = sem.shape[1], width // sem.shape[1]
    edge = edges.shape[1]
    loads = []
    for part in range(parts):
        span = pl.ds(part * columns, columns)
        for index, source in enumerate(sources):
            target = held.at[index] if index < 3 else edges.at[index - 3]
            loads.append(pltpu.make_async_copy(source.at[:, span], target.at[:, span], sem.at[index, part]))
            loads[-1].start()
    total = rows + 2 * edge
    time_tile = lax.axis_index("seq") // tiles_across
    later = time_tile % 2 == 0
    row_frame = lax.broadcasted_iota(jnp.int32, (rows, total), 0) // PLANE
    column = lax.broadcasted_iota(jnp.int32, (rows, total), 1)
    pair_frame = (column - rows) // PLANE + jnp.where(later, TT, -HALO_F)
    far_frame = (column - rows - edge) // PLANE + jnp.where(later, -HALO_F, TT)
    key_frame = jnp.where(column < rows, column // PLANE, jnp.where(column < rows + edge, pair_frame, far_frame))
    absolute = key_frame + time_tile * TT
    distance = jnp.where((absolute >= 0) & (absolute < NT * TT), jnp.abs(row_frame - key_frame), FAR)
    for limit in range(HALO_F):
        bias[limit] = jnp.where(distance <= limit + 1, 0.0, MASKED)
    heads = columns // HD
    for head in range(width // HD):
        if head % heads == 0:
            for load in loads[head // heads * len(sources) : (head // heads + 1) * len(sources)]:
                load.wait()
        cut = head_cut(head)
        keys = jnp.concatenate([held[1, :, cut], edges[0, :, cut], edges[2, :, cut]], axis=0)
        values = jnp.concatenate([held[2, :, cut], edges[1, :, cut], edges[3, :, cut]], axis=0)
        scores = dot_rows(held[0, :, cut], keys) * SCALE + bias[reach[head] - 1]
        out_ref[:, cut] = blend(scores, values)


def attend_window(head_reach, fine_query, fine_key, fine_value, halo, tiles_across):
    rows, width = fine_query.shape
    kind = fine_query.dtype
    sources = (fine_query, fine_key, fine_value, *halo)
    parts = 4 if width % (4 * HD) == 0 else 1
    return pl.pallas_call(
        functools.partial(window_kernel, tiles_across),
        out_shape=jax.ShapeDtypeStruct((rows, width), jnp.float32),
        in_specs=[SMEM] + [HBM] * 3 + [ANY] * len(halo),
        out_specs=VMEM,
        scratch_shapes=[
            pltpu.VMEM((3, rows, width), kind),
            pltpu.VMEM((4,) + halo[0].shape, kind),
            pltpu.VMEM((HALO_F, rows, 2 * rows), jnp.float32),
            pltpu.SemaphoreType.DMA((len(sources), parts)),
        ],
        compiler_params=GRANT,
        name="attend_window",
    )(head_reach, *map(streamed, sources[:3]), *halo)


def finish_kernel(window_ref, coarse_ref, out_ref):
    rows = window_ref.shape[0]
    groups, coarse_rows, group_width = coarse_ref.shape
    row = lax.broadcasted_iota(jnp.int32, (rows, coarse_rows), 0)
    column = lax.broadcasted_iota(jnp.int32, (rows, coarse_rows), 1)
    frame, y, x = row // PLANE, (row % PLANE) // TW, row % TW
    source = frame * CELLS + (y // 2) * (TW // 2) + x // 2
    pick = (source == column).astype(jnp.bfloat16)
    for group in range(groups):
        cut = slice(group * group_width, (group + 1) * group_width)
        out_ref[:, cut] = (window_ref[:, cut] + dot_plain(pick, coarse_ref[group])).astype(out_ref.dtype)


def finish(window, returned):
    return pl.pallas_call(
        finish_kernel,
        out_shape=jax.ShapeDtypeStruct(window.shape, jnp.bfloat16),
        in_specs=[VMEM, VMEM],
        out_specs=VMEM,
        compiler_params=GRANT,
        name="finish",
    )(resident(window), resident(returned))


def shards(coarse_query, coarse_key, coarse_value, fine_query, fine_key, fine_value, head_reach):
    devices = lax.axis_size("seq")
    head_count = coarse_query.shape[1] // HD
    groups = math.gcd(head_count, devices)
    blocks = devices // groups
    inner = math.gcd(2, groups)
    outer = groups // inner
    tiles_across = devices // NT

    def seat(o, b, c):
        return (o * blocks + b) * inner + c

    def around(value, extent, move):
        moved = []
        for step in range(1, extent):
            links = [
                (seat(o, b, c), seat(*move(o, b, c, step)))
                for o in range(outer)
                for b in range(blocks)
                for c in range(inner)
            ]
            moved.append(lax.ppermute(value, "seq", links))
        return moved

    over_blocks = functools.partial(around, extent=blocks, move=lambda o, b, c, s: (o, (b + s) % blocks, c))
    over_outer = functools.partial(around, extent=outer, move=lambda o, b, c, s: ((o + s) % outer, b, c))
    over_inner = functools.partial(around, extent=inner, move=lambda o, b, c, s: (o, b, (c + s) % inner))
    same_block = [[seat(o, b, c) for o in range(outer) for c in range(inner)] for b in range(blocks)]

    def exchange(slots):
        return lax.all_to_all(slots, "seq", 0, 0, tiled=True, axis_index_groups=same_block)

    def between_tiles(value, move):
        ends = [(t, t + move(t)) for t in range(NT)]
        links = [
            (a * tiles_across + r, b * tiles_across + r)
            for a, b in ends
            if 0 <= b < NT
            for r in range(tiles_across)
        ]
        return lax.ppermute(value, "seq", links)

    def to_pair(value):
        return between_tiles(value, lambda t: 1 - 2 * (t % 2))

    def to_far(value):
        return between_tiles(value, lambda t: 2 * (t % 2) - 1)

    def to_next_pair(value):
        return between_tiles(value, lambda t: 2 - 4 * (t % 2))

    slots, pooled, pair_key, pair_value, far_key, far_value = pack(
        coarse_query, coarse_key, coarse_value, fine_key, fine_value, groups, tiles_across
    )
    pieces = [pooled] + over_blocks(pooled)
    far_value = to_pair(far_value)
    pair_key = to_pair(pair_key)
    received = exchange(slots)
    token_part = split_pooled(pieces)
    pieces = [token_part] + over_outer(token_part)
    tokens = jnp.concatenate(pieces, axis=0)
    all_tokens = [tokens] + over_inner(tokens)
    coarse_rows = coarse_query.shape[0]
    coarse_keys = received[:, coarse_rows:]
    others = over_blocks(coarse_keys)
    pair_value = to_pair(pair_value)
    far_value = to_next_pair(far_value)
    far_key = to_far(far_key)
    halo = (pair_key, pair_value, far_key, far_value)
    cross_result = attend_cross(fine_query, all_tokens, token_part.shape[0])
    attended = attend_coarse(received, others)
    returned = exchange(attended)
    head_reach, cross_result = lax.optimization_barrier((head_reach, cross_result))
    window = attend_window(head_reach, fine_query, fine_key, fine_value, halo, tiles_across)
    fine_result = finish(window, returned)
    return (fine_result, cross_result)


def solution(mesh):
    rows = P(("group", "seq"), None)
    return jax.shard_map(
        shards, mesh=mesh, in_specs=(rows,) * 6 + (P(),), out_specs=(rows, rows), check_vma=False
    )
```

```python
import functools
import math

import jax
import jax.numpy as jnp
from jax import lax
from jax.experimental import pallas as pl
from jax.experimental.pallas import tpu as pltpu
from jax.sharding import PartitionSpec as P


HD = 128
TT = 4
TH = 4
TW = 8
NT = 8
HALO_F = 2

PLANE = TH * TW
CELLS = (TH // 2) * (TW // 2)
SCALE = HD**-0.5
MASKED = -1e30
FAR = 1 << 20
GRANT = pltpu.CompilerParams(vmem_limit_bytes=12 << 20)


VMEM = pl.BlockSpec(memory_space=pltpu.VMEM)
SMEM = pl.BlockSpec(memory_space=pltpu.SMEM)
HBM = pl.BlockSpec(memory_space=pltpu.HBM)
ANY = pl.BlockSpec(memory_space=pl.ANY)


def streamed(value):
    return pltpu.with_memory_space_constraint(value, pltpu.HBM)


def resident(value):
    return pltpu.with_memory_space_constraint(value, pltpu.VMEM)


def dot_rows(left, right):
    return lax.dot_general(left, right, (((1,), (1,)), ((), ())), preferred_element_type=jnp.float32)


def dot_plain(left, right):
    return lax.dot_general(left, right, (((1,), (0,)), ((), ())), preferred_element_type=jnp.float32)


def blend(scores, values):
    exponent = jnp.exp(scores - jnp.max(scores, axis=-1, keepdims=True)).astype(jnp.bfloat16)
    ones = jnp.ones((values.shape[0], HD), values.dtype)
    sums = dot_plain(exponent, jnp.concatenate([values, ones], axis=1))
    return sums[:, :HD] * (1.0 / sums[:, HD:])


def head_cut(head):
    return slice(head * HD, (head + 1) * HD)


def pool_rows(rows):
    cells = rows.astype(jnp.float32).reshape(-1, CELLS, rows.shape[1])
    return jnp.sum(cells, axis=1) * CELLS**-0.5


def outer_slots(reach, heads):
    near, wide = jnp.int32(0), jnp.int32(0)
    slots = []
    for head in range(heads):
        is_wide = (reach[head] > 1).astype(jnp.int32)
        slots.append(pl.multiple_of(jnp.where(is_wide == 1, wide, heads - 1 - near) * HD, HD))
        wide += is_wide
        near += 1 - is_wide
    return slots


def sent_wide(heads):
    return max(1, heads * 2 // 3)


def pack_kernel(
    tiles_across,
    reach_hbm,
    query_hbm,
    key_hbm,
    value_hbm,
    fine_key_hbm,
    fine_value_hbm,
    slots_hbm,
    pooled_ref,
    pair_key_hbm,
    far_key_hbm,
    pair_value_hbm,
    far_value_hbm,
    pair_rest_hbm,
    far_rest_hbm,
    coarse_buf,
    fine_buf,
    outer_buf,
    reach,
    in_sem,
    slot_sem,
    edge_sem,
):
    groups = slots_hbm.shape[0]
    rows, width = query_hbm.shape
    fine_rows = fine_key_hbm.shape[0]
    group_width = width // groups
    heads = width // HD
    kept = sent_wide(heads) * HD
    odd = (lax.axis_index("seq") // tiles_across) % 2
    loads = []
    for index, source in enumerate((fine_key_hbm, fine_value_hbm)):
        loads.append(pltpu.make_async_copy(source, fine_buf.at[index], in_sem.at[index]))
    for index, source in enumerate((query_hbm, key_hbm, value_hbm)):
        loads.append(pltpu.make_async_copy(source, coarse_buf.at[index], in_sem.at[2 + index]))
    reach_load = pltpu.make_async_copy(reach_hbm, reach, in_sem.at[5])
    reach_load.start()
    for load in loads:
        load.start()
    reach_load.wait()
    stores = []

    def send(source, target, sem):
        stores.append(pltpu.make_async_copy(source, target, sem))
        stores[-1].start()

    slots = outer_slots(reach, heads)
    sides = ((pair_key_hbm, far_key_hbm), (pair_value_hbm, far_value_hbm))
    for index in range(2):
        loads[index].wait()
        for side, last in enumerate((1 - odd, odd)):
            start = pl.multiple_of(last * (fine_rows - PLANE), PLANE)
            send(
                fine_buf.at[index, pl.ds(start, PLANE)],
                sides[index][side].at[:, pl.ds(0, width)],
                edge_sem.at[index, side, 0],
            )
        for head in range(heads):
            cut = head_cut(head)
            span = pl.ds(slots[head], HD)
            outer_buf[index, 1 - odd, :, span] = fine_buf[index, PLANE : 2 * PLANE, cut]
            outer_buf[index, odd, :, span] = fine_buf[index, fine_rows - 2 * PLANE : fine_rows - PLANE, cut]
        for side, rest in enumerate((pair_rest_hbm, far_rest_hbm)):
            send(
                outer_buf.at[index, side, :, pl.ds(0, kept)],
                sides[index][side].at[:, pl.ds(width, kept)],
                edge_sem.at[index, side, 1],
            )
            send(
                outer_buf.at[index, side, :, pl.ds(kept, width - kept)],
                rest.at[:, pl.ds(index * (width - kept), width - kept)],
                edge_sem.at[index, side, 2],
            )
    for index in range(3):
        loads[2 + index].wait()
        for group in range(groups):
            stores.append(
                pltpu.make_async_copy(
                    coarse_buf.at[index, :, pl.ds(group * group_width, group_width)],
                    slots_hbm.at[group, pl.ds(index * rows, rows)],
                    slot_sem.at[index, group],
                )
            )
            stores[-1].start()
    pooled_ref[:TT] = pool_rows(coarse_buf[1])
    pooled_ref[TT:] = pool_rows(coarse_buf[2])
    for store in stores:
        store.wait()


def pack(head_reach, coarse_query, coarse_key, coarse_value, fine_key, fine_value, groups, tiles_across):
    rows, width = coarse_query.shape
    kind = coarse_query.dtype
    kept = sent_wide(width // HD) * HD
    halo = pltpu.HBM((PLANE, width + kept), kind)
    rest = pltpu.HBM((PLANE, 2 * (width - kept)), kind)
    return pl.pallas_call(
        functools.partial(pack_kernel, tiles_across),
        out_shape=(
            pltpu.HBM((groups, 3 * rows, width // groups), kind),
            jax.ShapeDtypeStruct((2 * TT, width), jnp.float32),
            halo,
            halo,
            halo,
            halo,
            rest,
            rest,
        ),
        in_specs=[HBM] * 6,
        out_specs=(HBM, VMEM) + (HBM,) * 6,
        scratch_shapes=[
            pltpu.VMEM((3, rows, width), kind),
            pltpu.VMEM((2,) + fine_key.shape, kind),
            pltpu.VMEM((2, 2, PLANE, width), kind),
            pltpu.SMEM(head_reach.shape, head_reach.dtype),
            pltpu.SemaphoreType.DMA((6,)),
            pltpu.SemaphoreType.DMA((3, groups)),
            pltpu.SemaphoreType.DMA((2, 2, 3)),
        ],
        compiler_params=GRANT,
        name="pack",
    )(*map(streamed, (head_reach, coarse_query, coarse_key, coarse_value, fine_key, fine_value)))


def split_pooled_kernel(*refs):
    *in_refs, out_ref = refs
    keys = jnp.concatenate([ref[:TT] for ref in in_refs], axis=0)
    values = jnp.concatenate([ref[TT:] for ref in in_refs], axis=0)
    high = keys.astype(jnp.bfloat16).astype(jnp.float32)
    out_ref[...] = jnp.concatenate([high, keys - high, values], axis=0).astype(jnp.bfloat16)


def split_pooled(pieces):
    width = pieces[0].shape[1]
    return pl.pallas_call(
        split_pooled_kernel,
        out_shape=jax.ShapeDtypeStruct((3 * TT * len(pieces), width), jnp.bfloat16),
        in_specs=[VMEM] * len(pieces),
        out_specs=VMEM,
        compiler_params=GRANT,
        name="split_pooled",
    )(*pieces)


def coarse_kernel(own_ref, *refs):
    *other_refs, out_ref = refs
    members, packed, group_width = own_ref.shape
    rows = packed // 3
    for head in range(group_width // HD):
        cut = head_cut(head)

        def flat(ref, start):
            return ref[:, start : start + rows, cut].reshape(members * rows, HD)

        query = flat(own_ref, 0)
        keys = jnp.concatenate([flat(own_ref, rows)] + [flat(r, 0) for r in other_refs], axis=0)
        values = jnp.concatenate([flat(own_ref, 2 * rows)] + [flat(r, rows) for r in other_refs], axis=0)
        mixed = blend(dot_rows(query, keys) * SCALE, values)
        out_ref[:, :, cut] = mixed.astype(out_ref.dtype).reshape(members, rows, HD)


def attend_coarse(own, others):
    members, packed, group_width = own.shape
    return pl.pallas_call(
        coarse_kernel,
        out_shape=jax.ShapeDtypeStruct((members, packed // 3, group_width), own.dtype),
        in_specs=[VMEM] * (1 + len(others)),
        out_specs=VMEM,
        compiler_params=GRANT,
        name="attend_coarse",
    )(own, *others)


def cross_kernel(query_ref, *refs):
    *token_refs, out_ref = refs
    third = token_refs[0].shape[0] // 3
    for head in range(query_ref.shape[1] // HD):
        cut = head_cut(head)
        high, low, values = (
            jnp.concatenate([ref[part * third : (part + 1) * third, cut] for ref in token_refs], axis=0)
            for part in range(3)
        )
        query = query_ref[:, cut]
        scores = dot_rows(jnp.concatenate([query, query], axis=1), jnp.concatenate([high, low], axis=1))
        out_ref[:, cut] = blend(scores * SCALE, values).astype(out_ref.dtype)


def attend_cross(fine_query, tokens):
    rows, width = fine_query.shape
    columns = width // 2 if width % (2 * HD) == 0 else width
    return pl.pallas_call(
        cross_kernel,
        out_shape=jax.ShapeDtypeStruct(fine_query.shape, jnp.bfloat16),
        grid=(width // columns,),
        in_specs=[pl.BlockSpec((t.shape[0], columns), lambda c: (0, c)) for t in (fine_query, *tokens)],
        out_specs=pl.BlockSpec((rows, columns), lambda c: (0, c)),
        compiler_params=GRANT,
        name="attend_cross",
    )(streamed(fine_query), *tokens)


def window_kernel(tiles_across, reach, *refs):
    query_hbm, key_hbm, value_hbm, *halo, pair_rest, far_rest, out_ref, held, inner, outer, bias, sem, outer_sem = refs
    rows, width = out_ref.shape
    heads = width // HD
    kept = sent_wide(heads) * HD
    parts = sem.shape[1]
    columns = width // parts
    outers = []
    for index in range(4):
        rest = (pair_rest, far_rest)[index % 2].at[:, pl.ds(index // 2 * (width - kept), width - kept)]
        outers.append(
            pltpu.make_async_copy(
                halo[index].at[:, pl.ds(width, kept)], outer.at[index, :, pl.ds(0, kept)], outer_sem.at[index, 0]
            )
        )
        outers.append(
            pltpu.make_async_copy(rest, outer.at[index, :, pl.ds(kept, width - kept)], outer_sem.at[index, 1])
        )
    for load in outers:
        load.start()
    loads = []
    for part in range(parts):
        span = pl.ds(part * columns, columns)
        for index, source in enumerate((query_hbm, key_hbm, value_hbm, *halo)):
            target = held.at[index] if index < 3 else inner.at[index - 3]
            loads.append(pltpu.make_async_copy(source.at[:, span], target.at[:, span], sem.at[index, part]))
            loads[-1].start()
    slots = outer_slots(reach, heads)
    total = 2 * rows
    time_tile = lax.axis_index("seq") // tiles_across
    later = time_tile % 2 == 0
    row_frame = lax.broadcasted_iota(jnp.int32, (rows, total), 0) // PLANE
    column = lax.broadcasted_iota(jnp.int32, (rows, total), 1)
    beyond = jnp.maximum(column - rows, 0) // PLANE
    depth = beyond % HALO_F
    after = (beyond < HALO_F) == later
    key_frame = jnp.where(column < rows, column // PLANE, jnp.where(after, TT + depth, -1 - depth))
    absolute = key_frame + time_tile * TT
    distance = jnp.where((absolute >= 0) & (absolute < NT * TT), jnp.abs(row_frame - key_frame), FAR)
    for limit in range(HALO_F):
        bias[limit] = jnp.where(distance <= limit + 1, 0.0, MASKED)
    for load in outers:
        load.wait()
    chunk = columns // HD
    for head in range(heads):
        if head % chunk == 0:
            for load in loads[head // chunk * 7 : (head // chunk + 1) * 7]:
                load.wait()
        cut = head_cut(head)
        span = pl.ds(slots[head], HD)

        def gathered(own, kind):
            pieces = [held[own, :, cut]]
            for side in (kind, kind + 1):
                pieces += [inner[side, :, cut], outer[side, :, span]]
            return jnp.concatenate(pieces, axis=0)

        scores = dot_rows(held[0, :, cut], gathered(1, 0)) * SCALE + bias[reach[head] - 1]
        out_ref[:, cut] = blend(scores, gathered(2, 2))


def attend_window(head_reach, fine_query, fine_key, fine_value, halo, rest, tiles_across):
    rows, width = fine_query.shape
    kind = fine_query.dtype
    parts = 4 if width % (4 * HD) == 0 else 1
    return pl.pallas_call(
        functools.partial(window_kernel, tiles_across),
        out_shape=jax.ShapeDtypeStruct((rows, width), jnp.float32),
        in_specs=[SMEM] + [HBM] * 3 + [ANY] * 6,
        out_specs=VMEM,
        scratch_shapes=[
            pltpu.VMEM((3, rows, width), kind),
            pltpu.VMEM((4, PLANE, width), kind),
            pltpu.VMEM((4, PLANE, width), kind),
            pltpu.VMEM((HALO_F, rows, 2 * rows), jnp.float32),
            pltpu.SemaphoreType.DMA((7, parts)),
            pltpu.SemaphoreType.DMA((4, 2)),
        ],
        compiler_params=GRANT,
        name="attend_window",
    )(head_reach, *map(streamed, (fine_query, fine_key, fine_value)), *halo, *rest)


def finish_kernel(window_ref, coarse_ref, out_ref):
    rows = window_ref.shape[0]
    groups, coarse_rows, group_width = coarse_ref.shape
    row = lax.broadcasted_iota(jnp.int32, (rows, coarse_rows), 0)
    column = lax.broadcasted_iota(jnp.int32, (rows, coarse_rows), 1)
    frame, y, x = row // PLANE, (row % PLANE) // TW, row % TW
    source = frame * CELLS + (y // 2) * (TW // 2) + x // 2
    pick = (source == column).astype(jnp.bfloat16)
    for group in range(groups):
        cut = slice(group * group_width, (group + 1) * group_width)
        out_ref[:, cut] = (window_ref[:, cut] + dot_plain(pick, coarse_ref[group])).astype(out_ref.dtype)


def finish(window, returned):
    return pl.pallas_call(
        finish_kernel,
        out_shape=jax.ShapeDtypeStruct(window.shape, jnp.bfloat16),
        in_specs=[VMEM, VMEM],
        out_specs=VMEM,
        compiler_params=GRANT,
        name="finish",
    )(resident(window), resident(returned))


def shards(coarse_query, coarse_key, coarse_value, fine_query, fine_key, fine_value, head_reach):
    devices = lax.axis_size("seq")
    head_count = coarse_query.shape[1] // HD
    groups = math.gcd(head_count, devices)
    blocks = devices // groups
    inner = math.gcd(2, groups)
    outer = groups // inner
    tiles_across = devices // NT

    def seat(o, b, c):
        return (o * blocks + b) * inner + c

    def around(value, extent, move):
        moved = []
        for step in range(1, extent):
            links = [
                (seat(o, b, c), seat(*move(o, b, c, step)))
                for o in range(outer)
                for b in range(blocks)
                for c in range(inner)
            ]
            moved.append(lax.ppermute(value, "seq", links))
        return moved

    over_blocks = functools.partial(around, extent=blocks, move=lambda o, b, c, s: (o, (b + s) % blocks, c))
    over_outer = functools.partial(around, extent=outer, move=lambda o, b, c, s: ((o + s) % outer, b, c))
    over_inner = functools.partial(around, extent=inner, move=lambda o, b, c, s: (o, b, (c + s) % inner))
    same_block = [[seat(o, b, c) for o in range(outer) for c in range(inner)] for b in range(blocks)]

    def exchange(slots):
        return lax.all_to_all(slots, "seq", 0, 0, tiled=True, axis_index_groups=same_block)

    def between_tiles(value, move):
        ends = [(t, t + move(t)) for t in range(NT)]
        links = [
            (a * tiles_across + r, b * tiles_across + r)
            for a, b in ends
            if 0 <= b < NT
            for r in range(tiles_across)
        ]
        return lax.ppermute(value, "seq", links)

    def to_pair(value):
        return between_tiles(value, lambda t: 1 - 2 * (t % 2))

    def to_far(value):
        return between_tiles(value, lambda t: 2 * (t % 2) - 1)

    def to_next_pair(value):
        return between_tiles(value, lambda t: 2 - 4 * (t % 2))

    slots, pooled, pair_key, far_key, pair_value, far_value, *rest = pack(
        head_reach, coarse_query, coarse_key, coarse_value, fine_key, fine_value, groups, tiles_across
    )
    pieces = [pooled] + over_blocks(pooled)
    far_value = to_pair(far_value)
    pair_key = to_pair(pair_key)
    received = exchange(slots)
    token_part = split_pooled(pieces)
    pieces = [token_part] + over_outer(token_part)
    third = token_part.shape[0] // 3
    tokens = jnp.concatenate([p[k * third : (k + 1) * third] for k in range(3) for p in pieces], axis=0)
    all_tokens = [tokens] + over_inner(tokens)
    coarse_rows = coarse_query.shape[0]
    coarse_keys = received[:, coarse_rows:]
    others = over_blocks(coarse_keys)
    pair_value = to_pair(pair_value)
    far_value = to_next_pair(far_value)
    far_key = to_far(far_key)
    rest = lax.cond(
        jnp.sum((head_reach > 1).astype(jnp.int32)) > sent_wide(head_count),
        lambda pair, far: (to_pair(pair), to_far(far)),
        lambda pair, far: (pair, far),
        *rest,
    )
    halo = (pair_key, far_key, pair_value, far_value)
    cross_result = attend_cross(fine_query, all_tokens)
    attended = attend_coarse(received, others)
    returned = exchange(attended)
    head_reach, cross_result = lax.optimization_barrier((head_reach, cross_result))
    window = attend_window(head_reach, fine_query, fine_key, fine_value, halo, rest, tiles_across)
    fine_result = finish(window, returned)
    return (fine_result, cross_result)


def solution(mesh):
    rows = P(("group", "seq"), None)
    return jax.shard_map(
        shards, mesh=mesh, in_specs=(rows,) * 6 + (P(),), out_specs=(rows, rows), check_vma=False
    )
```

```python
import functools
import math

import jax
import jax.numpy as jnp
from jax import lax
from jax.experimental import pallas as pl
from jax.experimental.pallas import tpu as pltpu
from jax.sharding import PartitionSpec as P


HD = 128
TT = 4
TH = 4
TW = 8
NT = 8
HALO_F = 2

PLANE = TH * TW
CELLS = (TH // 2) * (TW // 2)
SCALE = HD**-0.5
MASKED = -1e30
FAR = 1 << 20
GRANT = pltpu.CompilerParams(vmem_limit_bytes=12 << 20)


VMEM = pl.BlockSpec(memory_space=pltpu.VMEM)
SMEM = pl.BlockSpec(memory_space=pltpu.SMEM)
HBM = pl.BlockSpec(memory_space=pltpu.HBM)


def streamed(value):
    return pltpu.with_memory_space_constraint(value, pltpu.HBM)


def resident(value):
    return pltpu.with_memory_space_constraint(value, pltpu.VMEM)


def dot_rows(left, right):
    return lax.dot_general(left, right, (((1,), (1,)), ((), ())), preferred_element_type=jnp.float32)


def dot_plain(left, right):
    return lax.dot_general(left, right, (((1,), (0,)), ((), ())), preferred_element_type=jnp.float32)


def blend(scores, values):
    exponent = jnp.exp(scores - jnp.max(scores, axis=-1, keepdims=True)).astype(jnp.bfloat16)
    ones = jnp.ones((values.shape[0], HD), values.dtype)
    sums = dot_plain(exponent, jnp.concatenate([values, ones], axis=1))
    return sums[:, :HD] * (1.0 / sums[:, HD:])


def head_cut(head):
    return slice(head * HD, (head + 1) * HD)


def pool_rows(rows):
    cells = rows.astype(jnp.float32).reshape(-1, CELLS, rows.shape[1])
    return jnp.sum(cells, axis=1) * CELLS**-0.5


def outer_slots(reach, heads):
    near, wide = jnp.int32(0), jnp.int32(0)
    slots = []
    for head in range(heads):
        is_wide = (reach[head] > 1).astype(jnp.int32)
        slots.append(pl.multiple_of(jnp.where(is_wide == 1, wide, heads - 1 - near) * HD, HD))
        wide += is_wide
        near += 1 - is_wide
    return slots


def sent_wide(heads):
    return max(1, heads * 2 // 3)


def pack_kernel(
    tiles_across,
    reach_hbm,
    query_hbm,
    key_hbm,
    value_hbm,
    fine_key_hbm,
    fine_value_hbm,
    slots_hbm,
    pooled_ref,
    pair_key_hbm,
    far_key_hbm,
    pair_value_hbm,
    far_value_hbm,
    pair_rest_hbm,
    far_rest_hbm,
    coarse_buf,
    fine_buf,
    outer_buf,
    reach,
    in_sem,
    slot_sem,
    edge_sem,
):
    groups = slots_hbm.shape[0]
    rows, width = query_hbm.shape
    fine_rows = fine_key_hbm.shape[0]
    group_width = width // groups
    heads = width // HD
    kept = sent_wide(heads) * HD
    odd = (lax.axis_index("seq") // tiles_across) % 2
    loads = []
    for index, source in enumerate((fine_key_hbm, fine_value_hbm)):
        loads.append(pltpu.make_async_copy(source, fine_buf.at[index], in_sem.at[index]))
    for index, source in enumerate((query_hbm, key_hbm, value_hbm)):
        loads.append(pltpu.make_async_copy(source, coarse_buf.at[index], in_sem.at[2 + index]))
    reach_load = pltpu.make_async_copy(reach_hbm, reach, in_sem.at[5])
    reach_load.start()
    for load in loads:
        load.start()
    reach_load.wait()
    stores = []

    def send(source, target, sem):
        stores.append(pltpu.make_async_copy(source, target, sem))
        stores[-1].start()

    slots = outer_slots(reach, heads)
    sides = ((pair_key_hbm, far_key_hbm), (pair_value_hbm, far_value_hbm))
    for index in range(2):
        loads[index].wait()
        for side, last in enumerate((1 - odd, odd)):
            start = pl.multiple_of(last * (fine_rows - PLANE), PLANE)
            send(
                fine_buf.at[index, pl.ds(start, PLANE)],
                sides[index][side].at[:, pl.ds(0, width)],
                edge_sem.at[index, side, 0],
            )
        for head in range(heads):
            cut = head_cut(head)
            span = pl.ds(slots[head], HD)
            outer_buf[index, 1 - odd, :, span] = fine_buf[index, PLANE : 2 * PLANE, cut]
            outer_buf[index, odd, :, span] = fine_buf[index, fine_rows - 2 * PLANE : fine_rows - PLANE, cut]
        for side, rest in enumerate((pair_rest_hbm, far_rest_hbm)):
            send(
                outer_buf.at[index, side, :, pl.ds(0, kept)],
                sides[index][side].at[:, pl.ds(width, kept)],
                edge_sem.at[index, side, 1],
            )
            send(
                outer_buf.at[index, side, :, pl.ds(kept, width - kept)],
                rest.at[:, pl.ds(index * (width - kept), width - kept)],
                edge_sem.at[index, side, 2],
            )
    for index in range(3):
        loads[2 + index].wait()
        for group in range(groups):
            stores.append(
                pltpu.make_async_copy(
                    coarse_buf.at[index, :, pl.ds(group * group_width, group_width)],
                    slots_hbm.at[group, pl.ds(index * rows, rows)],
                    slot_sem.at[index, group],
                )
            )
            stores[-1].start()
    pooled_ref[:TT] = pool_rows(coarse_buf[1])
    pooled_ref[TT:] = pool_rows(coarse_buf[2])
    for store in stores:
        store.wait()


def pack(head_reach, coarse_query, coarse_key, coarse_value, fine_key, fine_value, groups, tiles_across):
    rows, width = coarse_query.shape
    kind = coarse_query.dtype
    kept = sent_wide(width // HD) * HD
    halo = pltpu.HBM((PLANE, width + kept), kind)
    rest = pltpu.HBM((PLANE, 2 * (width - kept)), kind)
    return pl.pallas_call(
        functools.partial(pack_kernel, tiles_across),
        out_shape=(
            pltpu.HBM((groups, 3 * rows, width // groups), kind),
            jax.ShapeDtypeStruct((2 * TT, width), jnp.float32),
            halo,
            halo,
            halo,
            halo,
            rest,
            rest,
        ),
        in_specs=[HBM] * 6,
        out_specs=(HBM, VMEM) + (HBM,) * 6,
        scratch_shapes=[
            pltpu.VMEM((3, rows, width), kind),
            pltpu.VMEM((2,) + fine_key.shape, kind),
            pltpu.VMEM((2, 2, PLANE, width), kind),
            pltpu.SMEM(head_reach.shape, head_reach.dtype),
            pltpu.SemaphoreType.DMA((6,)),
            pltpu.SemaphoreType.DMA((3, groups)),
            pltpu.SemaphoreType.DMA((2, 2, 3)),
        ],
        compiler_params=GRANT,
        name="pack",
    )(*map(streamed, (head_reach, coarse_query, coarse_key, coarse_value, fine_key, fine_value)))


def split_pooled_kernel(*refs):
    *in_refs, out_ref = refs
    keys = jnp.concatenate([ref[:TT] for ref in in_refs], axis=0)
    values = jnp.concatenate([ref[TT:] for ref in in_refs], axis=0)
    high = keys.astype(jnp.bfloat16).astype(jnp.float32)
    out_ref[...] = jnp.concatenate([high, keys - high, values], axis=0).astype(jnp.bfloat16)


def split_pooled(pieces):
    width = pieces[0].shape[1]
    return pl.pallas_call(
        split_pooled_kernel,
        out_shape=jax.ShapeDtypeStruct((3 * TT * len(pieces), width), jnp.bfloat16),
        in_specs=[VMEM] * len(pieces),
        out_specs=VMEM,
        compiler_params=GRANT,
        name="split_pooled",
    )(*pieces)


def coarse_kernel(own_ref, *refs):
    *other_refs, out_ref = refs
    members, packed, group_width = own_ref.shape
    rows = packed // 3
    for head in range(group_width // HD):
        cut = head_cut(head)

        def flat(ref, start):
            return ref[:, start : start + rows, cut].reshape(members * rows, HD)

        query = flat(own_ref, 0)
        keys = jnp.concatenate([flat(own_ref, rows)] + [flat(r, 0) for r in other_refs], axis=0)
        values = jnp.concatenate([flat(own_ref, 2 * rows)] + [flat(r, rows) for r in other_refs], axis=0)
        mixed = blend(dot_rows(query, keys) * SCALE, values)
        out_ref[:, :, cut] = mixed.astype(out_ref.dtype).reshape(members, rows, HD)


def attend_coarse(own, others):
    members, packed, group_width = own.shape
    return pl.pallas_call(
        coarse_kernel,
        out_shape=jax.ShapeDtypeStruct((members, packed // 3, group_width), own.dtype),
        in_specs=[VMEM] * (1 + len(others)),
        out_specs=VMEM,
        compiler_params=GRANT,
        name="attend_coarse",
    )(own, *others)


def merge_kernel(*refs):
    *in_refs, out_ref = refs
    third = in_refs[0].shape[0] // 3
    parts = [ref[...].astype(jnp.float32) for ref in in_refs]
    rows = [p[k * third : (k + 1) * third] for k in range(3) for p in parts]
    out_ref[...] = jnp.concatenate(rows, axis=0).astype(out_ref.dtype)


def merge_tokens(pieces):
    rows, width = pieces[0].shape
    return pl.pallas_call(
        merge_kernel,
        out_shape=jax.ShapeDtypeStruct((rows * len(pieces), width), pieces[0].dtype),
        in_specs=[VMEM] * len(pieces),
        out_specs=VMEM,
        compiler_params=GRANT,
        name="merge_tokens",
    )(*pieces)


def cross_kernel(query_ref, *refs):
    *token_refs, out_ref = refs
    third = token_refs[0].shape[0] // 3
    for head in range(query_ref.shape[1] // HD):
        cut = head_cut(head)
        high, low, values = (
            jnp.concatenate([ref[part * third : (part + 1) * third, cut] for ref in token_refs], axis=0)
            for part in range(3)
        )
        query = query_ref[:, cut]
        scores = dot_rows(jnp.concatenate([query, query], axis=1), jnp.concatenate([high, low], axis=1))
        out_ref[:, cut] = blend(scores * SCALE, values).astype(out_ref.dtype)


def attend_cross(fine_query, tokens):
    return pl.pallas_call(
        cross_kernel,
        out_shape=jax.ShapeDtypeStruct(fine_query.shape, jnp.bfloat16),
        in_specs=[VMEM] * (1 + len(tokens)),
        out_specs=VMEM,
        compiler_params=GRANT,
        name="attend_cross",
    )(*map(resident, (fine_query, *tokens)))


def hold_kernel(*refs):
    count = len(refs) // 2
    *refs, sem = refs
    loads = [pltpu.make_async_copy(refs[i], refs[count + i], sem.at[i]) for i in range(count)]
    for load in loads:
        load.start()
    for load in loads:
        load.wait()


def hold(*values):
    return pl.pallas_call(
        hold_kernel,
        out_shape=tuple(pltpu.VMEM(v.shape, v.dtype) for v in values),
        in_specs=[HBM] * len(values),
        out_specs=(VMEM,) * len(values),
        scratch_shapes=[pltpu.SemaphoreType.DMA((len(values),))],
        compiler_params=GRANT,
        name="hold",
    )(*map(streamed, values))


def window_kernel(tiles_across, reach, query_ref, key_ref, value_ref, *refs):
    *halo, pair_rest, far_rest, out_ref, outer, bias = refs
    rows, width = out_ref.shape
    heads = width // HD
    kept = sent_wide(heads) * HD
    for index in range(4):
        rest = (pair_rest, far_rest)[index % 2]
        start = index // 2 * (width - kept)
        outer[index, :, :kept] = halo[index][:, width:]
        outer[index, :, kept:] = rest[:, start : start + width - kept]
    slots = outer_slots(reach, heads)
    total = 2 * rows
    time_tile = lax.axis_index("seq") // tiles_across
    later = time_tile % 2 == 0
    row_frame = lax.broadcasted_iota(jnp.int32, (rows, total), 0) // PLANE
    column = lax.broadcasted_iota(jnp.int32, (rows, total), 1)
    beyond = jnp.maximum(column - rows, 0) // PLANE
    depth = beyond % HALO_F
    after = (beyond < HALO_F) == later
    key_frame = jnp.where(column < rows, column // PLANE, jnp.where(after, TT + depth, -1 - depth))
    absolute = key_frame + time_tile * TT
    distance = jnp.where((absolute >= 0) & (absolute < NT * TT), jnp.abs(row_frame - key_frame), FAR)
    for limit in range(HALO_F):
        bias[limit] = jnp.where(distance <= limit + 1, 0.0, MASKED)
    for head in range(heads):
        cut = head_cut(head)
        span = pl.ds(slots[head], HD)

        def gathered(own, kind):
            pieces = [own[:, cut]]
            for side in (kind, kind + 1):
                pieces += [halo[side][:, cut], outer[side, :, span]]
            return jnp.concatenate(pieces, axis=0)

        scores = dot_rows(query_ref[:, cut], gathered(key_ref, 0)) * SCALE + bias[reach[head] - 1]
        out_ref[:, cut] = blend(scores, gathered(value_ref, 2))


def attend_window(head_reach, fine_query, fine_key, fine_value, halo, rest, tiles_across):
    rows, width = fine_query.shape
    return pl.pallas_call(
        functools.partial(window_kernel, tiles_across),
        out_shape=jax.ShapeDtypeStruct((rows, width), jnp.float32),
        in_specs=[SMEM] + [VMEM] * 9,
        out_specs=VMEM,
        scratch_shapes=[
            pltpu.VMEM((4, PLANE, width), fine_query.dtype),
            pltpu.VMEM((HALO_F, rows, 2 * rows), jnp.float32),
        ],
        compiler_params=GRANT,
        name="attend_window",
    )(head_reach, *map(resident, (fine_query, fine_key, fine_value, *halo)), *rest)


def finish_kernel(window_ref, coarse_ref, out_ref):
    rows = window_ref.shape[0]
    groups, coarse_rows, group_width = coarse_ref.shape
    row = lax.broadcasted_iota(jnp.int32, (rows, coarse_rows), 0)
    column = lax.broadcasted_iota(jnp.int32, (rows, coarse_rows), 1)
    frame, y, x = row // PLANE, (row % PLANE) // TW, row % TW
    source = frame * CELLS + (y // 2) * (TW // 2) + x // 2
    pick = (source == column).astype(jnp.bfloat16)
    for group in range(groups):
        cut = slice(group * group_width, (group + 1) * group_width)
        out_ref[:, cut] = (window_ref[:, cut] + dot_plain(pick, coarse_ref[group])).astype(out_ref.dtype)


def finish(window, returned):
    return pl.pallas_call(
        finish_kernel,
        out_shape=jax.ShapeDtypeStruct(window.shape, jnp.bfloat16),
        in_specs=[VMEM, VMEM],
        out_specs=VMEM,
        compiler_params=GRANT,
        name="finish",
    )(resident(window), resident(returned))


def shards(coarse_query, coarse_key, coarse_value, fine_query, fine_key, fine_value, head_reach):
    devices = lax.axis_size("seq")
    head_count = coarse_query.shape[1] // HD
    groups = math.gcd(head_count, devices)
    blocks = devices // groups
    inner = math.gcd(2, groups)
    outer = groups // inner
    tiles_across = devices // NT

    def seat(o, b, c):
        return (o * blocks + b) * inner + c

    def around(value, extent, move):
        moved = []
        for step in range(1, extent):
            links = [
                (seat(o, b, c), seat(*move(o, b, c, step)))
                for o in range(outer)
                for b in range(blocks)
                for c in range(inner)
            ]
            moved.append(lax.ppermute(value, "seq", links))
        return moved

    over_blocks = functools.partial(around, extent=blocks, move=lambda o, b, c, s: (o, (b + s) % blocks, c))
    over_outer = functools.partial(around, extent=outer, move=lambda o, b, c, s: ((o + s) % outer, b, c))
    over_inner = functools.partial(around, extent=inner, move=lambda o, b, c, s: (o, b, (c + s) % inner))
    same_block = [[seat(o, b, c) for o in range(outer) for c in range(inner)] for b in range(blocks)]

    def exchange(slots):
        return lax.all_to_all(slots, "seq", 0, 0, tiled=True, axis_index_groups=same_block)

    def between_tiles(value, move):
        ends = [(t, t + move(t)) for t in range(NT)]
        links = [
            (a * tiles_across + r, b * tiles_across + r)
            for a, b in ends
            if 0 <= b < NT
            for r in range(tiles_across)
        ]
        return lax.ppermute(value, "seq", links)

    def to_pair(value):
        return between_tiles(value, lambda t: 1 - 2 * (t % 2))

    def to_far(value):
        return between_tiles(value, lambda t: 2 * (t % 2) - 1)

    def to_next_pair(value):
        return between_tiles(value, lambda t: 2 - 4 * (t % 2))

    slots, pooled, pair_key, far_key, pair_value, far_value, *rest = pack(
        head_reach, coarse_query, coarse_key, coarse_value, fine_key, fine_value, groups, tiles_across
    )
    fine_query, fine_key, fine_value = hold(fine_query, fine_key, fine_value)
    pieces = [pooled] + over_blocks(pooled)
    far_value = to_pair(far_value)
    pair_key = to_pair(pair_key)
    received = exchange(slots)
    token_part = split_pooled(pieces)
    pieces = [token_part] + over_outer(token_part)
    tokens = merge_tokens(pieces)
    all_tokens = [tokens] + over_inner(tokens)
    coarse_rows = coarse_query.shape[0]
    coarse_keys = received[:, coarse_rows:]
    others = over_blocks(coarse_keys)
    pair_value = to_pair(pair_value)
    far_value = to_next_pair(far_value)
    far_key = to_far(far_key)
    rest = lax.cond(
        jnp.sum((head_reach > 1).astype(jnp.int32)) > sent_wide(head_count),
        lambda pair, far: (to_pair(pair), to_far(far)),
        lambda pair, far: (pair, far),
        *rest,
    )
    halo = (pair_key, far_key, pair_value, far_value)
    cross_result = attend_cross(fine_query, all_tokens)
    attended = attend_coarse(received, others)
    returned = exchange(attended)
    head_reach, cross_result = lax.optimization_barrier((head_reach, cross_result))
    window = attend_window(head_reach, fine_query, fine_key, fine_value, halo, rest, tiles_across)
    fine_result = finish(window, returned)
    return (fine_result, cross_result)


def solution(mesh):
    rows = P(("group", "seq"), None)
    return jax.shard_map(
        shards, mesh=mesh, in_specs=(rows,) * 6 + (P(),), out_specs=(rows, rows), check_vma=False
    )
```
